1024 devices in a mesh: phase: 32 (over x, z_hi, core), ctx: 8 (over y), tp: 4 (over z_lo).
Axes of the slice: x: 8, y: 8, z: 8 (z_hi: 2, z_lo: 4; z = z_hi * 4 + z_lo), core: 2. Of those that a mesh axis runs over, the one named last changes fastest.
Arguments:
- queries: bfloat16 [32, 1024, 4096], P('phase', 'ctx', 'tp'), may hold values from -8 to 8
- keys: bfloat16 [32, 1024, 512], P('phase', 'ctx', 'tp'), may hold values from -8 to 8
- values: bfloat16 [32, 1024, 512], P('phase', 'ctx', 'tp'), may hold values from -6 to 6
- seg_ids: int32 [32, 1024], P('phase'), may hold values from 0 to 3, never falling along the last dimension, each value on 1 to 512 neighbouring positions
- out_weight: bfloat16 [4096, 8192], P('tp', 'ctx'), may hold values from -0.5 to 0.5
- embedded: bfloat16 [1024, 8192], P('tp', 'ctx'), may hold values from -6 to 6
- hidden_prev: bfloat16 [32, 1024, 8192], P('phase', 'tp', 'ctx'), may hold values from -6 to 6
Outputs:
- hidden_next: bfloat16 [32, 1024, 8192], P('phase', 'tp', 'ctx')
The draws below stay inside these ranges and needn't reach their ends.
Inputs may be any that keep to these rules, and one draw needn't show every extreme that they name: `seg_ids`: within each section the segment number never falls; a segment holds at most 512 tokens.
All inputs are finite; a program needn't handle non-finite values.
Results may differ from the reference program's by a relative error of at most 0.015.
Values may be sent and summed in bfloat16 or wider, within the bound.
A program may use at most 32 MiB of HBM per device.

```python
import math
import jax
import jax.numpy as jnp
import numpy as np
from jax import lax

D = 8192
HEADS = 32
KV_HEADS = 4
HEAD_DIM = 128
SEGS = 4
S_SEC = 1024
SECTIONS = 32
SEG_MOST = 512
N_TP = 4


def base_block(key, salt, width):
    return jnp.clip(jax.random.normal(jax.random.fold_in(key, salt), (SECTIONS, S_SEC, width), jnp.float32), -8.0, 8.0)


def draw_queries(key, part):
    result = base_block(key, 1, HEADS * HEAD_DIM)
    return result.astype(jnp.bfloat16)


def draw_keys(key, part):
    result = base_block(key, 2, KV_HEADS * HEAD_DIM)
    return result.astype(jnp.bfloat16)


def block_levels(key, shape, shards, smallest, top_value):
    def one(axis_at, blocks):
        heights = jax.random.uniform(jax.random.fold_in(jax.random.fold_in(key, 6), axis_at), (blocks,), jnp.float32, smallest / len(shards), top_value / len(shards))
        return jnp.repeat(jnp.exp(heights), shape[axis_at] // blocks).reshape((-1,) + (1,) * (len(shape) - axis_at - 1))

    loudness = one(*shards[0])
    for cut in shards[1:]:
        loudness = loudness * one(*cut)
    return loudness


def length_profile(number_of, total, bound, lean):
    portions = [(1 << 20) // math.isqrt(standing ** lean) + 1 for standing in range(2, number_of + 1)]
    surplus, given = total - bound - (number_of - 1), [1] * (number_of - 1)
    while surplus > 0:
        movable = [i for i in range(number_of - 1) if given[i] < bound]
        mass, remaining = sum([portions[i] for i in movable]), surplus
        for i in movable:
            extra = min(bound - given[i], max(1, remaining * portions[i] // mass), surplus)
            given[i] = given[i] + extra
            surplus = surplus - extra
    return np.array([bound] + given)


def ragged_sizes(rng, count, total, most, slope):
    if count == 2:
        one = jax.random.randint(rng, (), max(1, total - most), min(most, total - 1) + 1)
        return jnp.stack([one, total - one])
    lengths = jnp.asarray(length_profile(count, total, most, slope), jnp.int32)
    twos = (count - 1) // 2
    giver, receiver = lengths[1:1 + 2 * twos:2], lengths[2:2 + 2 * twos:2]
    margin = jnp.minimum(giver - 1, most - receiver)
    passed = jax.random.randint(jax.random.fold_in(rng, 1), (twos,), 0, 1 << 20) % (margin + 1)
    lengths = lengths.at[1:1 + 2 * twos:2].set(giver - passed).at[2:2 + 2 * twos:2].set(receiver + passed)
    return lengths[jax.random.permutation(jax.random.fold_in(rng, 2), count)]


def noise(rng, extent, scale, limit, cuts=(), kind=jnp.bfloat16):
    factor_of = block_levels(rng, extent, cuts, -0.22, 0.18) if cuts else 1.0
    entries = jax.random.normal(rng, extent, jnp.float32) * scale * factor_of
    return jnp.minimum(jnp.maximum(entries, -limit), limit).astype(kind)


def setup_inputs(seed: int = 0) -> dict:
    splits = jax.random.split(jax.random.key(seed), 8)
    queries = draw_queries(jax.random.fold_in(splits[7], 71), 0)
    keys = draw_keys(jax.random.fold_in(splits[7], 71), 0)
    values = noise(splits[2], (SECTIONS, S_SEC, KV_HEADS * HEAD_DIM), 1.0, 6.0, ((0, 32), (1, 8), (2, 4)))
    seg_ids = jax.vmap(lambda own: jnp.searchsorted(jnp.cumsum(ragged_sizes(own, SEGS, S_SEC, SEG_MOST, 0)), jnp.arange(S_SEC), side="right"))(jax.random.split(splits[3], SECTIONS)).reshape((SECTIONS, S_SEC)).astype(jnp.int32)
    out_weight = noise(splits[4], (HEADS * HEAD_DIM, D), HEAD_DIM ** -0.5, 0.5, ((0, 4), (1, 8)))
    embedded = noise(splits[5], (S_SEC, D), 1.0, 6.0, ((0, 4), (1, 8)))
    hidden_prev = noise(splits[6], (SECTIONS, S_SEC, D), 1.0, 6.0, ((0, 32), (1, 4), (2, 8)))
    return {"queries": queries, "keys": keys, "values": values, "seg_ids": seg_ids, "out_weight": out_weight, "embedded": embedded, "hidden_prev": hidden_prev}


def attend(query_rows, key_rows, value_rows, segment_row):
    length = query_rows.shape[0]
    group_size = HEADS // KV_HEADS
    query_grid = query_rows.reshape(length, HEADS, HEAD_DIM)
    key_grid = key_rows.reshape(length, KV_HEADS, HEAD_DIM)
    value_grid = value_rows.reshape(length, KV_HEADS, HEAD_DIM)
    places = jnp.arange(length, dtype=jnp.int32)
    allowed = (places[:, None] >= places[None, :]) & (segment_row[:, None] == segment_row[None, :])
    score_scale = HEAD_DIM ** -0.5

    def one_head(head_index):
        kv_index = head_index // group_size
        query_head = query_grid[:, head_index, :]
        key_head = key_grid[:, kv_index, :]
        value_head = value_grid[:, kv_index, :]
        scores = jnp.dot(query_head, key_head.T, preferred_element_type=jnp.float32) * score_scale
        scores = jnp.where(allowed, scores, -1e30)
        row_max = jnp.max(scores, axis=1, keepdims=True)
        probs = jnp.where(allowed, jnp.exp(scores - row_max), 0.0)
        total = jnp.sum(probs, axis=1, keepdims=True)
        probs_low = probs.astype(jnp.bfloat16)
        return jnp.dot(probs_low, value_head, preferred_element_type=jnp.float32) / total

    heads_out = lax.map(one_head, jnp.arange(HEADS, dtype=jnp.int32))
    return jnp.transpose(heads_out, (1, 0, 2)).reshape(length, HEADS * HEAD_DIM).astype(jnp.bfloat16)


def reference(queries, keys, values, seg_ids, out_weight, embedded, hidden_prev):
    group_width = HEADS * HEAD_DIM // N_TP

    def section(section_index):
        attended = attend(queries[section_index], keys[section_index], values[section_index], seg_ids[section_index])
        branch = jnp.zeros((attended.shape[0], out_weight.shape[1]), jnp.float32)
        for group in range(N_TP):
            columns = attended[:, group * group_width:(group + 1) * group_width]
            rows = out_weight[group * group_width:(group + 1) * group_width, :]
            partial_value = jnp.dot(columns, rows, preferred_element_type=jnp.float32).astype(jnp.bfloat16)
            branch = branch + partial_value.astype(jnp.float32)
        before = hidden_prev[jnp.maximum(section_index - 1, 0)]
        resid_in = jnp.where(section_index == 0, embedded, before)
        return (resid_in.astype(jnp.float32) + branch).astype(jnp.bfloat16)

    return lax.map(section, jnp.arange(SECTIONS, dtype=jnp.int32))
```

```python
import jax
import jax.numpy as jnp
from jax import lax
from jax.experimental import pallas as pl
from jax.experimental.pallas import tpu as pltpu
from jax.sharding import PartitionSpec as P

HEAD_DIM = 128
BLOCK = 128
RING = 8
GROUP = 4
PIECE = 64
MASKED = -1e30
LOG2_E = 1.4426950408889634
F32 = jnp.float32
BF16 = jnp.bfloat16


def kernel(
    q_ref, k_ref, v_ref, seg_ref, w_ref, emb_ref, hp_ref, out_ref,
    qbuf, kv, bias, astage, aall, wall, hbuf, acc,
    local_sem, kv_s, kv_r, q_s, q_r, wz_s, wz_r, wx_s, wx_r, sib_s, sib_r, hid_s, hid_r, az_s, az_r, ay_s, ay_r,
):
    p = lax.axis_index("phase")
    y = lax.axis_index("ctx")
    z = lax.axis_index("tp")
    x = lax.div(p, 4)
    zh = lax.rem(lax.div(p, 2), 2)
    core = lax.rem(p, 2)
    zring = zh * GROUP + z

    def ring(value):
        return lax.rem(value + 2 * RING, RING)

    def at_y(step):
        return {"phase": p, "ctx": ring(y + step), "tp": z}

    def at_x(step):
        return {"phase": lax.rem(p + 4 * step + 32, 32), "ctx": y, "tp": z}

    def at_zring(step):
        there = ring(zring + step)
        return {"phase": x * 4 + lax.div(there, GROUP) * 2 + core, "ctx": y, "tp": lax.rem(there, GROUP)}

    def at_z(place):
        return {"phase": p, "ctx": y, "tp": place}

    def at_phase(step):
        return {"phase": lax.rem(p + step + 32, 32), "ctx": y, "tp": z}

    sibling = {"phase": p + 1 - 2 * core, "ctx": y, "tp": z}

    def remote(src, dst, send, recv, where):
        return pltpu.make_async_remote_copy(
            src_ref=src, dst_ref=dst, send_sem=send, recv_sem=recv,
            device_id=where, device_id_type=pl.DeviceIdType.MESH,
        )

    barrier = pltpu.get_barrier_semaphore()
    greeted = [at_y(d) for d in range(1, RING)]
    greeted += [at_z(lax.rem(z + d, GROUP)) for d in range(1, GROUP)]
    greeted += [at_zring(d) for d in (1, -1, 2, -2)]
    greeted += [at_x(1), at_x(-1), sibling, at_phase(1), at_phase(-1)]
    for peer in greeted:
        pl.semaphore_signal(barrier, inc=1, device_id=peer, device_id_type=pl.DeviceIdType.MESH)

    k_in = pltpu.make_async_copy(k_ref, kv.at[y, 0], local_sem.at[0])
    v_in = pltpu.make_async_copy(v_ref, kv.at[y, 1], local_sem.at[1])
    q_in = pltpu.make_async_copy(
        q_ref.at[:, pl.ds(pl.multiple_of(y * HEAD_DIM, HEAD_DIM), HEAD_DIM)], qbuf.at[y], local_sem.at[2]
    )
    w_in = pltpu.make_async_copy(w_ref, wall.at[:, z], local_sem.at[3])
    k_in.start()
    v_in.start()
    q_in.start()
    w_in.start()

    @pl.when(p == 0)
    def _():
        pltpu.make_async_copy(emb_ref, hbuf, local_sem.at[4]).start()

    k_in.wait()
    v_in.wait()
    pl.semaphore_wait(barrier, len(greeted))

    sends = []

    def go(copy):
        copy.start()
        sends.append(copy)

    def kv_copy(way, hop):
        block = ring(y - hop + 1) if way == 0 else ring(y + hop - 1)
        part = kv.at[block] if hop < 4 else kv.at[block, way]
        return remote(part, part, kv_s.at[way, hop - 1], kv_r.at[way, hop - 1], at_y(1 if way == 0 else -1))

    kv_copies = {(way, hop): kv_copy(way, hop) for way in (0, 1) for hop in (1, 2, 3, 4)}

    def kv_hop(hop):
        for way in (0, 1):
            go(kv_copies[way, hop])

    def kv_wait(hop):
        for way in (0, 1):
            kv_copies[way, hop].wait_recv()

    piece = pl.ds(pl.multiple_of(core * PIECE, PIECE), PIECE)
    half = PIECE // 2
    low = pl.ds(pl.multiple_of(core * PIECE, half), half)
    high = pl.ds(pl.multiple_of(core * PIECE + half, half), half)
    others = [lax.rem(z + 1, GROUP), lax.rem(z + 3, GROUP), lax.rem(z + 2, GROUP)]

    def wz_copy(index, rows, step):
        return remote(
            w_ref.at[x, rows], wall.at[x, z, rows], wz_s.at[index], wz_r.at[index], at_zring(step)
        )

    wz_copies = [wz_copy(0, piece, 1), wz_copy(1, piece, -1), wz_copy(2, low, 2), wz_copy(3, high, -2)]

    def wx_copy(way, hop, sub):
        block = ring(x - hop + 1) if way == 0 else ring(x + hop - 1)
        rows = piece
        if hop == 4 and sub == 2:
            rows = low if way == 0 else high
        part = wall.at[block, others[sub], rows]
        return remote(part, part, wx_s.at[way, hop - 1, sub], wx_r.at[way, hop - 1, sub], at_x(1 if way == 0 else -1))

    wx_copies = {
        (way, hop, sub): wx_copy(way, hop, sub)
        for way in (0, 1) for hop in (1, 2, 3, 4) for sub in (0, 1, 2)
        if hop < 4 or sub == 2 or sub == way
    }

    def sib_copy(slot, sub):
        hop = (slot + 1) // 2
        block = ring(x - hop) if slot % 2 else ring(x + hop)
        part = wall.at[block, others[sub], piece]
        return remote(part, part, sib_s.at[slot, sub], sib_r.at[slot, sub], sibling)

    sib_copies = {(slot, sub): sib_copy(slot, sub) for slot in range(8) for sub in range(3)}

    def wx_first(sub):
        go(wx_copies[0, 1, sub])
        go(wx_copies[1, 1, sub])
        go(sib_copies[0, sub])

    def wx_pass(hop, sub):
        for way in (0, 1):
            wx_copies[way, hop, sub].wait_recv()
            if (way, hop + 1, sub) in wx_copies:
                go(wx_copies[way, hop + 1, sub])
            go(sib_copies[2 * hop - 1 + way, sub])

    def wx_last():
        for sub in (0, 1, 2):
            for way in (0, 1):
                if (way, 4, sub) in wx_copies:
                    wx_copies[way, 4, sub].wait_recv()
            go(sib_copies[7, sub])

    def sib_wait(slots):
        for slot in slots:
            for sub in range(3):
                sib_copies[slot, sub].wait_recv()

    def hid_copy(part):
        rows = pl.ds(part * 128, 128)
        return remote(hp_ref.at[rows], hbuf.at[rows], hid_s.at[part], hid_r.at[part], at_phase(1))

    hid_copies = [hid_copy(0), hid_copy(1)]

    def hid_start(part):
        @pl.when(p < 31)
        def _():
            hid_copies[part].start()

    def q_copy(step):
        there = ring(y + step)
        return remote(
            q_ref.at[:, pl.ds(pl.multiple_of(there * HEAD_DIM, HEAD_DIM), HEAD_DIM)],
            qbuf.at[y], q_s.at[step], q_r.at[step], at_y(step),
        )

    q_copies = [q_copy(step) for step in (4, 3, 5, 2, 6, 1, 7)]

    kv_hop(1)
    for copy in wz_copies:
        go(copy)
    for copy in q_copies:
        go(copy)

    acc[...] = jnp.zeros_like(acc)
    row_iota = lax.broadcasted_iota(jnp.int32, (BLOCK, BLOCK), 0)
    col_iota = lax.broadcasted_iota(jnp.int32, (BLOCK, BLOCK), 1)
    for qi in range(RING):
        seg_rows = jnp.broadcast_to(seg_ref[:, qi * BLOCK:(qi + 1) * BLOCK], (BLOCK, BLOCK)).T
        first = max(0, qi - 4)
        for kj in range(first, qi + 1):
            allowed = seg_rows == seg_ref[:, kj * BLOCK:(kj + 1) * BLOCK]
            if kj == qi:
                allowed = allowed & (col_iota <= row_iota)
            bias[qi, :, (kj - first) * BLOCK:(kj - first + 1) * BLOCK] = jnp.where(allowed, 0.0, MASKED)

    kv_wait(1)
    kv_hop(2)
    wz_copies[1].wait_recv()
    wx_first(0)
    wz_copies[0].wait_recv()
    wx_first(1)
    kv_wait(2)
    kv_hop(3)
    wz_copies[2].wait_recv()
    wz_copies[3].wait_recv()
    wx_first(2)
    hid_start(0)
    kv_wait(3)
    kv_hop(4)
    q_in.wait()
    for copy in q_copies:
        copy.wait_recv()
    kv_wait(4)
    wx_pass(1, 0)

    def attend(qi):
        first = max(0, qi - 4)
        count = (qi + 1 - first) * BLOCK
        keys = kv[first:qi + 1, 0].reshape(count, HEAD_DIM)
        vals = kv[first:qi + 1, 1].reshape(count, HEAD_DIM)
        scores = lax.dot_general(qbuf[qi], keys, (((1,), (1,)), ((), ())), preferred_element_type=F32)
        scores = scores * (HEAD_DIM ** -0.5 * LOG2_E) + bias[qi, :, :count]
        top = jnp.max(scores, axis=1, keepdims=True)
        probs = jnp.exp2(scores - top)
        total = jnp.sum(probs, axis=1, keepdims=True)
        heads_out = jnp.dot(probs.astype(BF16), vals, preferred_element_type=F32) / total
        astage[qi // 2, (qi % 2) * BLOCK:(qi % 2 + 1) * BLOCK, :] = heads_out.astype(BF16)

    own_copy = pltpu.make_async_copy(astage.at[z], aall.at[y, z], local_sem.at[5])

    def az_copy(b):
        return remote(astage.at[b], aall.at[y, z], az_s.at[b], az_r.at[z], at_z(b))

    for order, b in enumerate((3, 0, 2, 1)):
        attend(2 * b)
        attend(2 * b + 1)

        @pl.when(z == b)
        def _():
            own_copy.start()

        @pl.when(z != b)
        def _():
            az_copy(b).start()

        if order == 1:
            wx_pass(1, 1)

    def ay_copy(way, hop, sub):
        block = ring(y - hop + 1) if way == 0 else ring(y + hop - 1)
        part = aall.at[block, sources[sub]]
        return remote(part, part, ay_s.at[way, hop - 1, sub], ay_r.at[way, hop - 1, sub], at_y(1 if way == 0 else -1))

    upper = lax.div(z, 2)
    sources = [z, z + 1 - 2 * lax.rem(z, 2), 2 - upper, 3 - 3 * upper]
    ay_copies = {
        (way, hop, sub): ay_copy(way, hop, sub)
        for way in (0, 1) for hop in (1, 2, 3, 4) for sub in range(4)
        if hop < 4 or sub // 2 == way
    }

    def ay_first(sub):
        if sub == 0:
            own_copy.wait()
        else:
            remote(astage.at[0], aall.at[y, sources[sub]], az_s.at[0], az_r.at[sources[sub]], sibling).wait_recv()
        go(ay_copies[0, 1, sub])
        go(ay_copies[1, 1, sub])

    def ay_pass(hop, sub):
        for way in (0, 1):
            ay_copies[way, hop, sub].wait_recv()
            if (way, hop + 1, sub) in ay_copies:
                go(ay_copies[way, hop + 1, sub])

    def apart(there, here):
        ahead = lax.rem(there - here + RING, RING)
        return jnp.minimum(ahead, RING - ahead)

    def project(reach, before):
        def one(block, carry):
            far = jnp.maximum(apart(block, y), apart(block, x))

            @pl.when((far <= reach) & (far > before))
            def _():
                left = jnp.concatenate([aall[block, g] for g in range(GROUP)], axis=1)
                for tile in range(4):
                    cols = slice(tile * 256, (tile + 1) * 256)
                    right = wall[block, :, :, cols].reshape(GROUP * BLOCK, 256)
                    acc[:, cols] += jnp.dot(left, right, preferred_element_type=F32)

            return carry

        lax.fori_loop(0, RING, one, 0)

    ay_first(0)
    ay_first(1)
    ay_first(2)
    ay_first(3)
    hid_start(1)
    wx_pass(1, 2)
    ay_pass(1, 0)
    wx_pass(2, 0)
    ay_pass(1, 1)
    ay_pass(1, 2)
    wx_pass(2, 1)
    ay_pass(1, 3)
    ay_pass(2, 0)
    wx_pass(2, 2)
    ay_pass(2, 1)
    ay_pass(2, 2)
    wx_pass(3, 0)
    ay_pass(2, 3)
    w_in.wait()
    sib_wait((0, 1, 2, 3, 4))
    project(2, -1)
    ay_pass(3, 0)
    wx_pass(3, 1)
    ay_pass(3, 1)
    ay_pass(3, 2)
    wx_pass(3, 2)
    ay_pass(3, 3)
    wx_last()
    sib_wait((5, 6))
    project(3, 2)
    for sub in range(4):
        ay_copies[sub // 2, 4, sub].wait_recv()
    sib_wait((7,))
    project(4, 3)

    @pl.when(p == 0)
    def _():
        pltpu.make_async_copy(emb_ref, hbuf, local_sem.at[4]).wait()

    @pl.when(p > 0)
    def _():
        for copy in hid_copies:
            copy.wait_recv()

    out_ref[...] = (hbuf[...].astype(F32) + acc[...]).astype(BF16)

    for copy in sends:
        copy.wait_send()
    for b in range(GROUP):
        @pl.when(z != b)
        def _():
            az_copy(b).wait_send()

    @pl.when(p < 31)
    def _():
        for copy in hid_copies:
            copy.wait_send()


def on_device(queries, keys, values, seg_ids, out_weight, embedded, hidden_prev):
    rows, width = embedded.shape
    dma = pltpu.SemaphoreType.DMA
    hbm = pl.BlockSpec(memory_space=pl.ANY)
    vmem = pl.BlockSpec(memory_space=pltpu.VMEM)
    result = pl.pallas_call(
        kernel,
        out_shape=jax.ShapeDtypeStruct((rows, width), BF16),
        in_specs=[hbm, hbm, hbm, vmem, hbm, hbm, hbm],
        out_specs=vmem,
        scratch_shapes=[
            pltpu.VMEM((RING, BLOCK, HEAD_DIM), BF16),
            pltpu.VMEM((RING, 2, BLOCK, HEAD_DIM), BF16),
            pltpu.VMEM((RING, BLOCK, 5 * BLOCK), F32),
            pltpu.VMEM((GROUP, 2 * BLOCK, HEAD_DIM), BF16),
            pltpu.VMEM((RING, GROUP, 2 * BLOCK, HEAD_DIM), BF16),
            pltpu.VMEM((RING, GROUP, BLOCK, width), BF16),
            pltpu.VMEM((rows, width), BF16),
            pltpu.VMEM((rows, width), F32),
            dma((6,)),
            dma((2, 4)), dma((2, 4)),
            dma((8,)), dma((8,)),
            dma((4,)), dma((4,)),
            dma((2, 4, 3)), dma((2, 4, 3)),
            dma((8, 3)), dma((8, 3)),
            dma((2,)), dma((2,)),
            dma((4,)), dma((4,)),
            dma((2, 4, 4)), dma((2, 4, 4)),
        ],
        compiler_params=pltpu.CompilerParams(
            collective_id=0, has_side_effects=True, vmem_limit_bytes=48 * 1024 * 1024
        ),
    )(
        queries[0], keys[0], values[0], seg_ids,
        out_weight.reshape(RING, BLOCK, out_weight.shape[1]), embedded, hidden_prev[0],
    )
    return result[None]


def solution(mesh):
    return jax.shard_map(
        on_device,
        mesh=mesh,
        in_specs=(
            P("phase", "ctx", "tp"),
            P("phase", "ctx", "tp"),
            P("phase", "ctx", "tp"),
            P("phase", None),
            P("tp", "ctx"),
            P("tp", "ctx"),
            P("phase", "tp", "ctx"),
        ),
        out_specs=P("phase", "tp", "ctx"),
        check_vma=False,
    )
```

```python
import jax
import jax.numpy as jnp
from jax import lax
from jax.experimental import pallas as pl
from jax.experimental.pallas import tpu as pltpu
from jax.sharding import PartitionSpec as P

HEAD_DIM = 128
BLOCK = 128
RING = 8
GROUP = 4
PIECE = 64
MASKED = -1e30
LOG2_E = 1.4426950408889634
F32 = jnp.float32
BF16 = jnp.bfloat16


def kernel(
    q_ref, k_ref, v_ref, seg_in, w_ref, emb_ref, hp_ref, out_ref,
    seg, qbuf, kv, bias, astage, aall, wall, hbuf, acc,
    ready, hid_ready, local_sem, kv_s, kv_r, q_s, q_r, wz_s, wz_r, wx_s, wx_r, sib_s, sib_r, hid_s, hid_r, az_s, az_r, ay_s, ay_r,
):
    p = lax.axis_index("phase")
    y = lax.axis_index("ctx")
    z = lax.axis_index("tp")
    x = lax.div(p, 4)
    zh = lax.rem(lax.div(p, 2), 2)
    core = lax.rem(p, 2)

    def ring(value):
        return lax.rem(value + 2 * RING, RING)

    def at_y(step):
        return {"phase": p, "ctx": ring(y + step), "tp": z}

    def at_x(step):
        return {"phase": lax.rem(p + 4 * step + 32, 32), "ctx": y, "tp": z}

    def at_z(place):
        return {"phase": p, "ctx": y, "tp": place}

    def at_phase(step):
        return {"phase": lax.rem(p + step + 32, 32), "ctx": y, "tp": z}

    sibling = {"phase": p + 1 - 2 * core, "ctx": y, "tp": z}

    def remote(src, dst, send, recv, where):
        return pltpu.make_async_remote_copy(
            src_ref=src, dst_ref=dst, send_sem=send, recv_sem=recv,
            device_id=where, device_id_type=pl.DeviceIdType.MESH,
        )

    def signal(sem, where):
        pl.semaphore_signal(sem, inc=1, device_id=where, device_id_type=pl.DeviceIdType.MESH)

    barrier = pltpu.get_barrier_semaphore()
    greeted = [at_y(d) for d in range(1, RING)] + [at_x(1), at_x(-1), sibling]
    for peer in greeted:
        signal(barrier, peer)
    for d in range(1, GROUP):
        @pl.when(z + d < GROUP)
        def _():
            signal(barrier, at_z(z + d))

    @pl.when(zh == 0)
    def _():
        signal(barrier, at_phase(2 * core - 1))

    k_in = pltpu.make_async_copy(k_ref, kv.at[y, 0], local_sem.at[0])
    v_in = pltpu.make_async_copy(v_ref, kv.at[y, 1], local_sem.at[1])
    q_in = pltpu.make_async_copy(
        q_ref.at[:, pl.ds(pl.multiple_of(y * HEAD_DIM, HEAD_DIM), HEAD_DIM)], qbuf.at[y], local_sem.at[2]
    )
    w_in = pltpu.make_async_copy(w_ref, wall.at[:, z], local_sem.at[3])
    k_in.start()
    v_in.start()
    q_in.start()
    seg_copy = pltpu.make_async_copy(seg_in, seg, local_sem.at[6])
    seg_copy.start()
    w_in.start()

    @pl.when(p == 0)
    def _():
        pltpu.make_async_copy(emb_ref, hbuf, local_sem.at[4]).start()

    k_in.wait()
    v_in.wait()
    pl.semaphore_wait(barrier, len(greeted) + z + zh)
    for d in range(1, GROUP):
        @pl.when(z - d >= 0)
        def _():
            signal(ready.at[z], at_z(z - d))

    @pl.when((zh == 1) & (core == 0))
    def _():
        signal(hid_ready, at_phase(-1))

    sends = []

    def go(copy):
        copy.start()
        sends.append(copy)

    def kv_copy(way, hop, part):
        block = ring(y - hop + 1) if way == 0 else ring(y + hop - 1)
        held = kv.at[block, part]
        return remote(
            held, held, kv_s.at[way, hop - 1, part], kv_r.at[way, hop - 1, part], at_y(1 if way == 0 else -1)
        )

    kv_copies = {
        (way, hop, part): kv_copy(way, hop, part)
        for way in (0, 1) for hop in (1, 2, 3, 4) for part in (0, 1)
        if hop < 4 or part == way
    }

    def kv_pass(hop):
        for part in (0, 1):
            for way in (0, 1):
                if (way, hop, part) in kv_copies:
                    kv_copies[way, hop, part].wait_recv()
                if (way, hop + 1, part) in kv_copies:
                    go(kv_copies[way, hop + 1, part])

    piece = pl.ds(pl.multiple_of(core * PIECE, PIECE), PIECE)
    half = PIECE // 2
    low = pl.ds(pl.multiple_of(core * PIECE, half), half)
    high = pl.ds(pl.multiple_of(core * PIECE + half, half), half)
    first = jnp.abs(z - 1)
    last = 3 - 3 * lax.div(z, 3)
    others = [first, 6 - z - first - last, last]
    sources = [z] + others

    def wz_copy(there):
        return remote(w_ref.at[x, piece], wall.at[x, z, piece], wz_s.at[there], wz_r.at[z], at_z(there))

    def wz_down():
        for d in range(1, GROUP):
            @pl.when(z - d >= 0)
            def _():
                wz_copy(z - d).start()

    def wz_up(d):
        @pl.when(z + d < GROUP)
        def _():
            pl.semaphore_wait(ready.at[z + d], 1)
            wz_copy(z + d).start()

    def wz_wait(sub):
        held = wall.at[x, others[sub], piece]
        remote(held, held, wz_s.at[others[sub]], wz_r.at[others[sub]], sibling).wait_recv()

    def wx_copy(way, hop, sub):
        block = ring(x - hop + 1) if way == 0 else ring(x + hop - 1)
        rows = piece
        if hop == 4 and sub == 2:
            rows = low if way == 0 else high
        part = wall.at[block, others[sub], rows]
        return remote(part, part, wx_s.at[way, hop - 1, sub], wx_r.at[way, hop - 1, sub], at_x(1 if way == 0 else -1))

    wx_copies = {
        (way, hop, sub): wx_copy(way, hop, sub)
        for way in (0, 1) for hop in (1, 2, 3, 4) for sub in (0, 1, 2)
        if hop < 4 or sub == 2 or sub == way
    }

    def sib_copy(slot, sub):
        hop = (slot + 1) // 2
        block = ring(x - hop) if slot % 2 else ring(x + hop)
        part = wall.at[block, others[sub], piece]
        return remote(part, part, sib_s.at[slot, sub], sib_r.at[slot, sub], sibling)

    sib_copies = {(slot, sub): sib_copy(slot, sub) for slot in range(8) for sub in range(3)}

    def wx_first(sub):
        go(wx_copies[0, 1, sub])
        go(wx_copies[1, 1, sub])
        go(sib_copies[0, sub])

    def wx_pass(hop, sub):
        for way in (0, 1):
            wx_copies[way, hop, sub].wait_recv()
            if (way, hop + 1, sub) in wx_copies:
                go(wx_copies[way, hop + 1, sub])
            go(sib_copies[2 * hop - 1 + way, sub])

    def wx_last():
        for sub in (0, 1, 2):
            for way in (0, 1):
                if (way, 4, sub) in wx_copies:
                    wx_copies[way, 4, sub].wait_recv()
            go(sib_copies[7, sub])

    def sib_wait(slots):
        for slot in slots:
            for sub in range(3):
                sib_copies[slot, sub].wait_recv()

    def hid_copy(part):
        rows = pl.ds(part * 128, 128)
        return remote(hp_ref.at[rows], hbuf.at[rows], hid_s.at[part], hid_r.at[part], at_phase(1))

    hid_copies = [hid_copy(0), hid_copy(1)]

    def hid_start(part):
        if part == 0:
            @pl.when((zh == 0) & (core == 1))
            def _():
                pl.semaphore_wait(hid_ready, 1)

        @pl.when(p < 31)
        def _():
            hid_copies[part].start()

    def q_copy(step):
        there = ring(y + step)
        return remote(
            q_ref.at[:, pl.ds(pl.multiple_of(there * HEAD_DIM, HEAD_DIM), HEAD_DIM)],
            qbuf.at[y], q_s.at[step], q_r.at[step], at_y(step),
        )

    q_copies = {step: q_copy(step) for step in range(1, RING)}

    for part in (0, 1):
        for way in (0, 1):
            go(kv_copies[way, 1, part])
    wz_down()
    go(q_copies[4])

    acc[...] = jnp.zeros_like(acc)
    seg_copy.wait()
    row_iota = lax.broadcasted_iota(jnp.int32, (BLOCK, BLOCK), 0)
    col_iota = lax.broadcasted_iota(jnp.int32, (BLOCK, BLOCK), 1)
    for qi in range(RING):
        seg_rows = jnp.broadcast_to(seg[:, qi * BLOCK:(qi + 1) * BLOCK], (BLOCK, BLOCK)).T
        low_key = max(0, qi - 4)
        for kj in range(low_key, qi + 1):
            allowed = seg_rows == seg[:, kj * BLOCK:(kj + 1) * BLOCK]
            if kj == qi:
                allowed = allowed & (col_iota <= row_iota)
            bias[qi, :, (kj - low_key) * BLOCK:(kj - low_key + 1) * BLOCK] = jnp.where(allowed, 0.0, MASKED)

    kv_pass(1)
    go(q_copies[3])
    go(q_copies[5])
    kv_pass(2)
    go(q_copies[2])
    go(q_copies[6])
    wz_up(1)
    kv_pass(3)
    go(q_copies[1])
    go(q_copies[7])
    wz_up(2)
    wz_wait(0)
    wx_first(0)
    q_in.wait()
    for copy in q_copies.values():
        copy.wait_recv()
    kv_pass(4)
    wz_up(3)
    wz_wait(1)
    wx_first(1)
    hid_start(0)

    def attend(qi):
        low_key = max(0, qi - 4)
        count = (qi + 1 - low_key) * BLOCK
        keys = kv[low_key:qi + 1, 0].reshape(count, HEAD_DIM)
        vals = kv[low_key:qi + 1, 1].reshape(count, HEAD_DIM)
        scores = lax.dot_general(qbuf[qi], keys, (((1,), (1,)), ((), ())), preferred_element_type=F32)
        scores = scores * (HEAD_DIM ** -0.5 * LOG2_E) + bias[qi, :, :count]
        top = jnp.max(scores, axis=1, keepdims=True)
        probs = jnp.exp2(scores - top)
        total = jnp.sum(probs, axis=1, keepdims=True)
        heads_out = jnp.dot(probs.astype(BF16), vals, preferred_element_type=F32) / total
        astage[qi // 2, (qi % 2) * BLOCK:(qi % 2 + 1) * BLOCK, :] = heads_out.astype(BF16)

    own_copy = pltpu.make_async_copy(astage.at[z], aall.at[y, z], local_sem.at[5])

    def az_copy(b):
        return remote(astage.at[b], aall.at[y, z], az_s.at[b], az_r.at[z], at_z(b))

    for b in range(GROUP):
        attend(2 * b)
        attend(2 * b + 1)

        @pl.when(z == b)
        def _():
            own_copy.start()

        @pl.when(z != b)
        def _():
            az_copy(b).start()

        if b == 0:
            wx_pass(1, 0)
        if b == 1:
            wz_wait(2)
            wx_first(2)
        if b == 3:
            wx_pass(1, 1)

    def ay_copy(way, hop, sub):
        block = ring(y - hop + 1) if way == 0 else ring(y + hop - 1)
        part = aall.at[block, sources[sub]]
        return remote(part, part, ay_s.at[way, hop - 1, sub], ay_r.at[way, hop - 1, sub], at_y(1 if way == 0 else -1))

    ay_copies = {
        (way, hop, sub): ay_copy(way, hop, sub)
        for way in (0, 1) for hop in (1, 2, 3, 4) for sub in range(4)
        if hop < 4 or sub // 2 == way
    }

    def ay_first(sub):
        if sub == 0:
            own_copy.wait()
        else:
            remote(astage.at[0], aall.at[y, sources[sub]], az_s.at[0], az_r.at[sources[sub]], sibling).wait_recv()
        go(ay_copies[0, 1, sub])
        go(ay_copies[1, 1, sub])

    def ay_pass(hop, sub):
        for way in (0, 1):
            ay_copies[way, hop, sub].wait_recv()
            if (way, hop + 1, sub) in ay_copies:
                go(ay_copies[way, hop + 1, sub])

    def apart(there, here):
        ahead = lax.rem(there - here + RING, RING)
        return jnp.minimum(ahead, RING - ahead)

    def project(reach, before):
        def one(block, carry):
            far = jnp.maximum(apart(block, y), apart(block, x))

            @pl.when((far <= reach) & (far > before))
            def _():
                left = jnp.concatenate([aall[block, g] for g in range(GROUP)], axis=1)
                for tile in range(4):
                    cols = slice(tile * 256, (tile + 1) * 256)
                    right = wall[block, :, :, cols].reshape(GROUP * BLOCK, 256)
                    acc[:, cols] += jnp.dot(left, right, preferred_element_type=F32)

            return carry

        lax.fori_loop(0, RING, one, 0)

    ay_first(0)
    wx_pass(1, 2)
    ay_first(1)
    wx_pass(2, 0)
    ay_pass(1, 0)
    ay_first(2)
    wx_pass(2, 1)
    ay_pass(1, 1)
    ay_first(3)
    hid_start(1)
    ay_pass(1, 2)
    wx_pass(2, 2)
    ay_pass(2, 0)
    ay_pass(1, 3)
    wx_pass(3, 0)
    ay_pass(2, 1)
    ay_pass(2, 2)
    wx_pass(3, 1)
    ay_pass(3, 0)
    ay_pass(2, 3)
    w_in.wait()
    sib_wait((0, 1, 2, 3, 4))
    project(2, -1)
    ay_pass(3, 1)
    ay_pass(3, 2)
    wx_pass(3, 2)
    ay_pass(3, 3)
    wx_last()
    sib_wait((5, 6))
    project(3, 2)
    for sub in range(4):
        ay_copies[sub // 2, 4, sub].wait_recv()
    sib_wait((7,))
    project(4, 3)

    @pl.when(p == 0)
    def _():
        pltpu.make_async_copy(emb_ref, hbuf, local_sem.at[4]).wait()

    @pl.when(p > 0)
    def _():
        for copy in hid_copies:
            copy.wait_recv()

    out_ref[...] = (hbuf[...].astype(F32) + acc[...]).astype(BF16)

    for copy in sends:
        copy.wait_send()
    for b in range(GROUP):
        @pl.when(z != b)
        def _():
            az_copy(b).wait_send()
            wz_copy(b).wait_send()

    @pl.when(p < 31)
    def _():
        for copy in hid_copies:
            copy.wait_send()


def on_device(queries, keys, values, seg_ids, out_weight, embedded, hidden_prev):
    rows, width = embedded.shape
    dma = pltpu.SemaphoreType.DMA
    hbm = pl.BlockSpec(memory_space=pltpu.HBM)
    vmem = pl.BlockSpec(memory_space=pltpu.VMEM)
    operands = (
        queries[0], keys[0], values[0], seg_ids,
        out_weight.reshape(RING, BLOCK, out_weight.shape[1]), embedded, hidden_prev[0],
    )
    result = pl.pallas_call(
        kernel,
        out_shape=jax.ShapeDtypeStruct((rows, width), BF16),
        in_specs=[hbm] * 7,
        out_specs=vmem,
        scratch_shapes=[
            pltpu.VMEM((1, RING * BLOCK), jnp.int32),
            pltpu.VMEM((RING, BLOCK, HEAD_DIM), BF16),
            pltpu.VMEM((RING, 2, BLOCK, HEAD_DIM), BF16),
            pltpu.VMEM((RING, BLOCK, 5 * BLOCK), F32),
            pltpu.VMEM((GROUP, 2 * BLOCK, HEAD_DIM), BF16),
            pltpu.VMEM((RING, GROUP, 2 * BLOCK, HEAD_DIM), BF16),
            pltpu.VMEM((RING, GROUP, BLOCK, width), BF16),
            pltpu.VMEM((rows, width), BF16),
            pltpu.VMEM((rows, width), F32),
            pltpu.SemaphoreType.REGULAR((GROUP,)), pltpu.SemaphoreType.REGULAR,
            dma((7,)),
            dma((2, 4, 2)), dma((2, 4, 2)),
            dma((8,)), dma((8,)),
            dma((4,)), dma((4,)),
            dma((2, 4, 3)), dma((2, 4, 3)),
            dma((8, 3)), dma((8, 3)),
            dma((2,)), dma((2,)),
            dma((4,)), dma((4,)),
            dma((2, 4, 4)), dma((2, 4, 4)),
        ],
        compiler_params=pltpu.CompilerParams(
            collective_id=0, has_side_effects=True, vmem_limit_bytes=48 * 1024 * 1024
        ),
    )(*(pltpu.with_memory_space_constraint(operand, pltpu.HBM) for operand in operands))
    return result[None]


def solution(mesh):
    return jax.shard_map(
        on_device,
        mesh=mesh,
        in_specs=(
            P("phase", "ctx", "tp"),
            P("phase", "ctx", "tp"),
            P("phase", "ctx", "tp"),
            P("phase", None),
            P("tp", "ctx"),
            P("tp", "ctx"),
            P("phase", "tp", "ctx"),
        ),
        out_specs=P("phase", "tp", "ctx"),
        check_vma=False,
    )
```

```python
import jax
import jax.numpy as jnp
from jax import lax
from jax.experimental import pallas as pl
from jax.experimental.pallas import tpu as pltpu
from jax.sharding import PartitionSpec as P

HEAD_DIM = 128
BLOCK = 128
RING = 8
GROUP = 4
PIECE = 64
MASKED = -1e30
LOG2_E = 1.4426950408889634
F32 = jnp.float32
BF16 = jnp.bfloat16


def kernel(
    q_ref, k_ref, v_ref, seg_in, w_ref, emb_ref, hp_ref, out_ref,
    seg, qbuf, kv, bias, astage, aall, wall, hbuf, acc,
    ready, hid_ready, local_sem, kv_s, kv_r, q_s, q_r, wz_s, wz_r, wx_s, wx_r, sib_s, sib_r, hid_s, hid_r, az_s, az_r, ay_s, ay_r,
):
    p = lax.axis_index("phase")
    y = lax.axis_index("ctx")
    z = lax.axis_index("tp")
    x = lax.div(p, 4)
    zh = lax.rem(lax.div(p, 2), 2)
    core = lax.rem(p, 2)

    def ring(value):
        return lax.rem(value + 2 * RING, RING)

    def at_y(step):
        return {"phase": p, "ctx": ring(y + step), "tp": z}

    def at_x(step):
        return {"phase": lax.rem(p + 4 * step + 32, 32), "ctx": y, "tp": z}

    def at_z(place):
        return {"phase": p, "ctx": y, "tp": place}

    def at_phase(step):
        return {"phase": lax.rem(p + step + 32, 32), "ctx": y, "tp": z}

    sibling = {"phase": p + 1 - 2 * core, "ctx": y, "tp": z}

    def remote(src, dst, send, recv, where):
        return pltpu.make_async_remote_copy(
            src_ref=src, dst_ref=dst, send_sem=send, recv_sem=recv,
            device_id=where, device_id_type=pl.DeviceIdType.MESH,
        )

    def signal(sem, where):
        pl.semaphore_signal(sem, inc=1, device_id=where, device_id_type=pl.DeviceIdType.MESH)

    barrier = pltpu.get_barrier_semaphore()
    greeted = [at_y(1), at_y(-1), at_x(1), at_x(-1), sibling]
    for peer in greeted:
        signal(barrier, peer)
    for d in range(1, GROUP):
        @pl.when(z + d < GROUP)
        def _():
            signal(barrier, at_z(z + d))

    @pl.when(zh == 0)
    def _():
        signal(barrier, at_phase(2 * core - 1))

    k_in = pltpu.make_async_copy(k_ref, kv.at[y, 0], local_sem.at[0])
    v_in = pltpu.make_async_copy(v_ref, kv.at[y, 1], local_sem.at[1])
    q_in = pltpu.make_async_copy(
        q_ref.at[:, pl.ds(pl.multiple_of(y * HEAD_DIM, HEAD_DIM), HEAD_DIM)], qbuf.at[y], local_sem.at[2]
    )
    w_in = pltpu.make_async_copy(w_ref, wall.at[:, z], local_sem.at[3])
    k_in.start()
    v_in.start()
    q_in.start()
    seg_copy = pltpu.make_async_copy(seg_in, seg, local_sem.at[6])
    seg_copy.start()
    w_in.start()

    @pl.when(p == 0)
    def _():
        pltpu.make_async_copy(emb_ref, hbuf, local_sem.at[4]).start()

    pl.semaphore_wait(barrier, len(greeted) + z + zh)
    for d in range(1, GROUP):
        @pl.when(z - d >= 0)
        def _():
            signal(ready.at[z], at_z(z - d))

    @pl.when((zh == 1) & (core == 0))
    def _():
        signal(hid_ready, at_phase(-1))

    sends = []

    def go(copy):
        copy.start()
        sends.append(copy)

    def kv_copy(way, hop, part):
        block = ring(y - hop + 1) if way == 0 else ring(y + hop - 1)
        held = kv.at[block, part]
        return remote(
            held if hop > 1 else (k_ref, v_ref)[part], held, kv_s.at[way, hop - 1, part], kv_r.at[way, hop - 1, part], at_y(1 if way == 0 else -1)
        )

    kv_copies = {
        (way, hop, part): kv_copy(way, hop, part)
        for way in (0, 1) for hop in (1, 2, 3, 4) for part in (0, 1)
        if hop < 4 or part == way
    }

    def kv_pass(hop):
        for part in (0, 1):
            for way in (0, 1):
                if (way, hop, part) in kv_copies:
                    kv_copies[way, hop, part].wait_recv()
                if (way, hop + 1, part) in kv_copies:
                    go(kv_copies[way, hop + 1, part])

    piece = pl.ds(pl.multiple_of(core * PIECE, PIECE), PIECE)
    half = PIECE // 2
    low = pl.ds(pl.multiple_of(core * PIECE, half), half)
    high = pl.ds(pl.multiple_of(core * PIECE + half, half), half)
    first = jnp.abs(z - 1)
    last = 3 - 3 * lax.div(z, 3)
    others = [first, 6 - z - first - last, last]
    sources = [z] + others

    def wz_copy(there):
        return remote(w_ref.at[x, piece], wall.at[x, z, piece], wz_s.at[there], wz_r.at[z], at_z(there))

    def wz_down():
        for d in range(1, GROUP):
            @pl.when(z - d >= 0)
            def _():
                wz_copy(z - d).start()

    def wz_up(d):
        @pl.when(z + d < GROUP)
        def _():
            pl.semaphore_wait(ready.at[z + d], 1)
            wz_copy(z + d).start()

    def wz_wait(sub):
        held = wall.at[x, others[sub], piece]
        remote(held, held, wz_s.at[others[sub]], wz_r.at[others[sub]], sibling).wait_recv()

    def wx_copy(way, hop, sub):
        block = ring(x - hop + 1) if way == 0 else ring(x + hop - 1)
        rows = piece
        if hop == 4 and sub == 2:
            rows = low if way == 0 else high
        part = wall.at[block, others[sub], rows]
        return remote(part, part, wx_s.at[way, hop - 1, sub], wx_r.at[way, hop - 1, sub], at_x(1 if way == 0 else -1))

    wx_copies = {
        (way, hop, sub): wx_copy(way, hop, sub)
        for way in (0, 1) for hop in (1, 2, 3, 4) for sub in (0, 1, 2)
        if hop < 4 or sub == 2 or sub == way
    }

    def sib_copy(slot, sub):
        hop = (slot + 1) // 2
        block = ring(x - hop) if slot % 2 else ring(x + hop)
        part = wall.at[block, others[sub], piece]
        return remote(part, part, sib_s.at[slot, sub], sib_r.at[slot, sub], sibling)

    sib_copies = {(slot, sub): sib_copy(slot, sub) for slot in range(8) for sub in range(3)}

    def wx_first(sub):
        go(wx_copies[0, 1, sub])
        go(wx_copies[1, 1, sub])
        go(sib_copies[0, sub])

    def wx_pass(hop, sub):
        for way in (0, 1):
            wx_copies[way, hop, sub].wait_recv()
            if (way, hop + 1, sub) in wx_copies:
                go(wx_copies[way, hop + 1, sub])
            go(sib_copies[2 * hop - 1 + way, sub])

    def wx_last():
        for sub in (0, 1, 2):
            for way in (0, 1):
                if (way, 4, sub) in wx_copies:
                    wx_copies[way, 4, sub].wait_recv()
            go(sib_copies[7, sub])

    def sib_wait(slots):
        for slot in slots:
            for sub in range(3):
                sib_copies[slot, sub].wait_recv()

    def hid_copy(part):
        rows = pl.ds(part * PIECE, PIECE)
        return remote(hp_ref.at[rows], hbuf.at[rows], hid_s.at[part], hid_r.at[part], at_phase(1))

    hid_copies = [hid_copy(part) for part in range(4)]

    def hid_start():
        @pl.when((zh == 0) & (core == 1))
        def _():
            pl.semaphore_wait(hid_ready, 1)

        @pl.when(p < 31)
        def _():
            for copy in hid_copies:
                copy.start()

    def q_copy(step):
        there = ring(y + step)
        return remote(
            q_ref.at[:, pl.ds(pl.multiple_of(there * HEAD_DIM, HEAD_DIM), HEAD_DIM)],
            qbuf.at[y], q_s.at[step], q_r.at[step], at_y(step),
        )

    q_copies = {step: q_copy(step) for step in range(1, RING)}

    for part in (0, 1):
        for way in (0, 1):
            go(kv_copies[way, 1, part])
    wz_down()
    go(q_copies[1])
    go(q_copies[7])

    acc[...] = jnp.zeros_like(acc)
    seg_copy.wait()
    row_iota = lax.broadcasted_iota(jnp.int32, (BLOCK, BLOCK), 0)
    col_iota = lax.broadcasted_iota(jnp.int32, (BLOCK, BLOCK), 1)
    for qi in range(RING):
        seg_rows = jnp.broadcast_to(seg[:, qi * BLOCK:(qi + 1) * BLOCK], (BLOCK, BLOCK)).T
        low_key = max(0, qi - 4)
        for kj in range(low_key, qi + 1):
            allowed = seg_rows == seg[:, kj * BLOCK:(kj + 1) * BLOCK]
            if kj == qi:
                allowed = allowed & (col_iota <= row_iota)
            bias[qi, :, (kj - low_key) * BLOCK:(kj - low_key + 1) * BLOCK] = jnp.where(allowed, 0.0, MASKED)

    kv_pass(1)
    go(q_copies[2])
    go(q_copies[6])
    wz_up(1)
    kv_pass(2)
    go(q_copies[3])
    go(q_copies[5])
    wz_wait(0)
    wx_first(0)
    wz_up(2)
    kv_pass(3)
    go(q_copies[4])
    wz_wait(1)
    wx_first(1)
    wz_up(3)
    kv_pass(4)
    wx_pass(1, 0)
    wz_wait(2)
    wx_first(2)
    k_in.wait()
    v_in.wait()
    q_in.wait()
    for copy in q_copies.values():
        copy.wait_recv()

    def attend(qi):
        low_key = max(0, qi - 4)
        count = (qi + 1 - low_key) * BLOCK
        keys = kv[low_key:qi + 1, 0].reshape(count, HEAD_DIM)
        vals = kv[low_key:qi + 1, 1].reshape(count, HEAD_DIM)
        scores = lax.dot_general(qbuf[qi], keys, (((1,), (1,)), ((), ())), preferred_element_type=F32)
        scores = scores * (HEAD_DIM ** -0.5 * LOG2_E) + bias[qi, :, :count]
        top = jnp.max(scores, axis=1, keepdims=True)
        probs = jnp.exp2(scores - top)
        total = jnp.sum(probs, axis=1, keepdims=True)
        heads_out = jnp.dot(probs.astype(BF16), vals, preferred_element_type=F32) / total
        astage[qi // 2, (qi % 2) * BLOCK:(qi % 2 + 1) * BLOCK, :] = heads_out.astype(BF16)

    own_copy = pltpu.make_async_copy(astage.at[z], aall.at[y, z], local_sem.at[5])

    def az_copy(b):
        return remote(astage.at[b], aall.at[y, z], az_s.at[b], az_r.at[z], at_z(b))

    for b in range(GROUP):
        attend(2 * b)
        attend(2 * b + 1)

        @pl.when(z == b)
        def _():
            own_copy.start()

        @pl.when(z != b)
        def _():
            az_copy(b).start()

        if b == 1:
            wx_pass(1, 1)

    def ay_copy(way, hop, sub):
        block = ring(y - hop + 1) if way == 0 else ring(y + hop - 1)
        part = aall.at[block, sources[sub]]
        return remote(part, part, ay_s.at[way, hop - 1, sub], ay_r.at[way, hop - 1, sub], at_y(1 if way == 0 else -1))

    ay_copies = {
        (way, hop, sub): ay_copy(way, hop, sub)
        for way in (0, 1) for hop in (1, 2, 3, 4) for sub in range(4)
        if hop < 4 or sub // 2 == way
    }

    def ay_first(sub):
        if sub == 0:
            own_copy.wait()
        else:
            remote(astage.at[0], aall.at[y, sources[sub]], az_s.at[0], az_r.at[sources[sub]], sibling).wait_recv()
        go(ay_copies[0, 1, sub])
        go(ay_copies[1, 1, sub])

    def ay_pass(hop, sub):
        for way in (0, 1):
            ay_copies[way, hop, sub].wait_recv()
            if (way, hop + 1, sub) in ay_copies:
                go(ay_copies[way, hop + 1, sub])

    def apart(there, here):
        ahead = lax.rem(there - here + RING, RING)
        return jnp.minimum(ahead, RING - ahead)

    def project(reach, before):
        def one(block, carry):
            far = jnp.maximum(apart(block, y), apart(block, x))

            @pl.when((far <= reach) & (far > before))
            def _():
                left = jnp.concatenate([aall[block, g] for g in range(GROUP)], axis=1)
                for tile in range(4):
                    cols = slice(tile * 256, (tile + 1) * 256)
                    right = wall[block, :, :, cols].reshape(GROUP * BLOCK, 256)
                    acc[:, cols] += jnp.dot(left, right, preferred_element_type=F32)

            return carry

        lax.fori_loop(0, RING, one, 0)

    ay_first(0)
    wx_pass(2, 0)
    wx_pass(1, 2)
    ay_first(1)
    ay_pass(1, 0)
    wx_pass(2, 1)
    ay_first(2)
    ay_pass(1, 1)
    wx_pass(3, 0)
    ay_pass(2, 0)
    wx_pass(2, 2)
    ay_pass(1, 2)
    ay_first(3)
    hid_start()
    ay_pass(2, 1)
    wx_pass(3, 1)
    ay_pass(2, 2)
    ay_pass(3, 0)
    ay_pass(1, 3)
    wx_pass(3, 2)
    ay_pass(3, 1)
    ay_pass(2, 3)
    w_in.wait()
    sib_wait((0, 1, 2, 3, 4))
    project(2, -1)
    ay_pass(3, 2)
    ay_pass(3, 3)
    wx_last()
    sib_wait((5, 6))
    project(3, 2)
    for sub in range(4):
        ay_copies[sub // 2, 4, sub].wait_recv()
    sib_wait((7,))
    project(4, 3)

    @pl.when(p == 0)
    def _():
        pltpu.make_async_copy(emb_ref, hbuf, local_sem.at[4]).wait()

    @pl.when(p > 0)
    def _():
        for copy in hid_copies:
            copy.wait_recv()

    out_ref[...] = (hbuf[...].astype(F32) + acc[...]).astype(BF16)

    for copy in sends:
        copy.wait_send()
    for b in range(GROUP):
        @pl.when(z != b)
        def _():
            az_copy(b).wait_send()
            wz_copy(b).wait_send()

    @pl.when(p < 31)
    def _():
        for copy in hid_copies:
            copy.wait_send()


def on_device(queries, keys, values, seg_ids, out_weight, embedded, hidden_prev):
    rows, width = embedded.shape
    dma = pltpu.SemaphoreType.DMA
    hbm = pl.BlockSpec(memory_space=pltpu.HBM)
    vmem = pl.BlockSpec(memory_space=pltpu.VMEM)
    operands = (
        queries[0], keys[0], values[0], seg_ids,
        out_weight.reshape(RING, BLOCK, out_weight.shape[1]), embedded, hidden_prev[0],
    )
    result = pl.pallas_call(
        kernel,
        out_shape=jax.ShapeDtypeStruct((rows, width), BF16),
        in_specs=[hbm] * 7,
        out_specs=vmem,
        scratch_shapes=[
            pltpu.VMEM((1, RING * BLOCK), jnp.int32),
            pltpu.VMEM((RING, BLOCK, HEAD_DIM), BF16),
            pltpu.VMEM((RING, 2, BLOCK, HEAD_DIM), BF16),
            pltpu.VMEM((RING, BLOCK, 5 * BLOCK), F32),
            pltpu.VMEM((GROUP, 2 * BLOCK, HEAD_DIM), BF16),
            pltpu.VMEM((RING, GROUP, 2 * BLOCK, HEAD_DIM), BF16),
            pltpu.VMEM((RING, GROUP, BLOCK, width), BF16),
            pltpu.VMEM((rows, width), BF16),
            pltpu.VMEM((rows, width), F32),
            pltpu.SemaphoreType.REGULAR((GROUP,)), pltpu.SemaphoreType.REGULAR,
            dma((7,)),
            dma((2, 4, 2)), dma((2, 4, 2)),
            dma((8,)), dma((8,)),
            dma((4,)), dma((4,)),
            dma((2, 4, 3)), dma((2, 4, 3)),
            dma((8, 3)), dma((8, 3)),
            dma((4,)), dma((4,)),
            dma((4,)), dma((4,)),
            dma((2, 4, 4)), dma((2, 4, 4)),
        ],
        compiler_params=pltpu.CompilerParams(
            collective_id=0, has_side_effects=True, vmem_limit_bytes=48 * 1024 * 1024
        ),
    )(*(pltpu.with_memory_space_constraint(operand, pltpu.HBM) for operand in operands))
    return result[None]


def solution(mesh):
    return jax.shard_map(
        on_device,
        mesh=mesh,
        in_specs=(
            P("phase", "ctx", "tp"),
            P("phase", "ctx", "tp"),
            P("phase", "ctx", "tp"),
            P("phase", None),
            P("tp", "ctx"),
            P("tp", "ctx"),
            P("phase", "tp", "ctx"),
        ),
        out_specs=P("phase", "tp", "ctx"),
        check_vma=False,
    )
```

```python
import jax
import jax.numpy as jnp
from jax import lax
from jax.experimental import pallas as pl
from jax.experimental.pallas import tpu as pltpu
from jax.sharding import PartitionSpec as P

HEAD_DIM = 128
BLOCK = 128
RING = 8
GROUP = 4
PIECE = 64
MASKED = -1e30
LOG2_E = 1.4426950408889634
F32 = jnp.float32
BF16 = jnp.bfloat16


def kernel(
    q_ref, k_ref, v_ref, seg_in, w_ref, emb_ref, hp_ref, out_ref,
    seg, qbuf, kv, bias, astage, aall, wall, hbuf, acc,
    ready, hid_ready, x_ready, sib_ready, local_sem, kv_s, kv_r, q_s, q_r, wz_s, wz_r, wx_s, wx_r, sib_s, sib_r, hid_s, hid_r, az_s, az_r, ay_s, ay_r,
):
    p = lax.axis_index("phase")
    y = lax.axis_index("ctx")
    z = lax.axis_index("tp")
    x = lax.div(p, 4)
    zh = lax.rem(lax.div(p, 2), 2)
    core = lax.rem(p, 2)

    def ring(value):
        return lax.rem(value + 2 * RING, RING)

    def at_y(step):
        return {"phase": p, "ctx": ring(y + step), "tp": z}

    def at_x(step):
        return {"phase": lax.rem(p + 4 * step + 32, 32), "ctx": y, "tp": z}

    def at_z(place):
        return {"phase": p, "ctx": y, "tp": place}

    def at_phase(step):
        return {"phase": lax.rem(p + step + 32, 32), "ctx": y, "tp": z}

    sibling = {"phase": p + 1 - 2 * core, "ctx": y, "tp": z}

    def remote(src, dst, send, recv, where):
        return pltpu.make_async_remote_copy(
            src_ref=src, dst_ref=dst, send_sem=send, recv_sem=recv,
            device_id=where, device_id_type=pl.DeviceIdType.MESH,
        )

    def signal(sem, where):
        pl.semaphore_signal(sem, inc=1, device_id=where, device_id_type=pl.DeviceIdType.MESH)

    barrier = pltpu.get_barrier_semaphore()
    lane = y + z + zh + core
    tail = (lane == 0) & (x == 0)
    beside = (lane == 0) & ((x == 1) | (x == RING - 1))
    for peer in (at_y(1), at_y(-1)):
        signal(barrier, peer)

    @pl.when(jnp.logical_not(tail))
    def _():
        for peer in (at_x(1), at_x(-1)):
            signal(barrier, peer)

    @pl.when(core == 1)
    def _():
        signal(barrier, sibling)

    for d in range(1, GROUP):
        @pl.when(z + d < GROUP)
        def _():
            signal(barrier, at_z(z + d))

    @pl.when(zh == 0)
    def _():
        signal(barrier, at_phase(2 * core - 1))

    k_in = pltpu.make_async_copy(k_ref, kv.at[y, 0], local_sem.at[0])
    v_in = pltpu.make_async_copy(v_ref, kv.at[y, 1], local_sem.at[1])
    q_in = pltpu.make_async_copy(
        q_ref.at[:, pl.ds(pl.multiple_of(y * HEAD_DIM, HEAD_DIM), HEAD_DIM)], qbuf.at[y], local_sem.at[2]
    )
    w_in = pltpu.make_async_copy(w_ref, wall.at[:, z], local_sem.at[3])
    k_in.start()
    v_in.start()
    q_in.start()
    seg_copy = pltpu.make_async_copy(seg_in, seg, local_sem.at[6])
    seg_copy.start()
    w_in.start()

    @pl.when(p == 0)
    def _():
        pltpu.make_async_copy(emb_ref, hbuf, local_sem.at[4]).start()

    awaited = 5 - core + z + zh - jnp.where(beside, 1, 0)
    pl.semaphore_wait(barrier, awaited)

    @pl.when(tail)
    def _():
        for peer in (at_x(1), at_x(-1)):
            signal(x_ready, peer)

    @pl.when(core == 0)
    def _():
        signal(sib_ready, sibling)

    for d in range(1, GROUP):
        @pl.when(z - d >= 0)
        def _():
            signal(ready.at[z], at_z(z - d))

    @pl.when((zh == 1) & (core == 0))
    def _():
        signal(hid_ready, at_phase(-1))

    sends = []

    def go(copy):
        copy.start()
        sends.append(copy)

    def kv_copy(way, hop, part):
        block = ring(y - hop + 1) if way == 0 else ring(y + hop - 1)
        held = kv.at[block, part]
        return remote(
            held if hop > 1 else (k_ref, v_ref)[part], held, kv_s.at[way, hop - 1, part], kv_r.at[way, hop - 1, part], at_y(1 if way == 0 else -1)
        )

    kv_copies = {
        (way, hop, part): kv_copy(way, hop, part)
        for way in (0, 1) for hop in (1, 2, 3, 4) for part in (0, 1)
        if hop < 4 or part == way
    }

    def kv_pass(hop):
        for part in (0, 1):
            for way in (0, 1):
                if (way, hop, part) in kv_copies:
                    kv_copies[way, hop, part].wait_recv()
                if (way, hop + 1, part) in kv_copies:
                    go(kv_copies[way, hop + 1, part])

    piece = pl.ds(pl.multiple_of(core * PIECE, PIECE), PIECE)
    half = PIECE // 2
    low = pl.ds(pl.multiple_of(core * PIECE, half), half)
    high = pl.ds(pl.multiple_of(core * PIECE + half, half), half)
    first = jnp.abs(z - 1)
    last = 3 - 3 * lax.div(z, 3)
    others = [first, 6 - z - first - last, last]
    sources = [z] + others

    def wz_copy(there):
        return remote(w_ref.at[x, piece], wall.at[x, z, piece], wz_s.at[there], wz_r.at[z], at_z(there))

    def wz_down():
        for d in range(1, GROUP):
            @pl.when(z - d >= 0)
            def _():
                wz_copy(z - d).start()

    def wz_up(d):
        @pl.when(z + d < GROUP)
        def _():
            pl.semaphore_wait(ready.at[z + d], 1)
            wz_copy(z + d).start()

    def wz_wait(sub):
        held = wall.at[x, others[sub], piece]
        remote(held, held, wz_s.at[others[sub]], wz_r.at[others[sub]], sibling).wait_recv()

    def wx_copy(way, hop, sub):
        block = ring(x - hop + 1) if way == 0 else ring(x + hop - 1)
        rows = piece
        if hop == 4 and sub == 2:
            rows = low if way == 0 else high
        part = wall.at[block, others[sub], rows]
        return remote(part, part, wx_s.at[way, hop - 1, sub], wx_r.at[way, hop - 1, sub], at_x(1 if way == 0 else -1))

    wx_copies = {
        (way, hop, sub): wx_copy(way, hop, sub)
        for way in (0, 1) for hop in (1, 2, 3, 4) for sub in (0, 1, 2)
        if hop < 4 or sub == 2 or sub == way
    }

    def sib_copy(slot, sub):
        hop = (slot + 1) // 2
        block = ring(x - hop) if slot % 2 else ring(x + hop)
        part = wall.at[block, others[sub], piece]
        return remote(part, part, sib_s.at[slot, sub], sib_r.at[slot, sub], sibling)

    sib_copies = {(slot, sub): sib_copy(slot, sub) for slot in range(8) for sub in range(3)}

    def wx_first(sub):
        go(wx_copies[0, 1, sub])
        go(wx_copies[1, 1, sub])
        go(sib_copies[0, sub])

    def wx_pass(hop, sub):
        for way in (0, 1):
            wx_copies[way, hop, sub].wait_recv()
            if (way, hop + 1, sub) in wx_copies:
                go(wx_copies[way, hop + 1, sub])
            go(sib_copies[2 * hop - 1 + way, sub])

    def wx_last():
        for sub in (0, 1, 2):
            for way in (0, 1):
                if (way, 4, sub) in wx_copies:
                    wx_copies[way, 4, sub].wait_recv()
            go(sib_copies[7, sub])

    def sib_wait(slots):
        for slot in slots:
            for sub in range(3):
                sib_copies[slot, sub].wait_recv()

    def hid_copy(part):
        rows = pl.ds(part * PIECE, PIECE)
        return remote(hp_ref.at[rows], hbuf.at[rows], hid_s.at[part], hid_r.at[part], at_phase(1))

    hid_copies = [hid_copy(part) for part in range(4)]

    def hid_start():
        @pl.when((zh == 0) & (core == 1))
        def _():
            pl.semaphore_wait(hid_ready, 1)

        @pl.when(p < 31)
        def _():
            for copy in hid_copies:
                copy.start()

    def q_copy(step):
        there = ring(y + step)
        return remote(
            q_ref.at[:, pl.ds(pl.multiple_of(there * HEAD_DIM, HEAD_DIM), HEAD_DIM)],
            qbuf.at[y], q_s.at[step], q_r.at[step], at_y(step),
        )

    q_copies = {step: q_copy(step) for step in range(1, RING)}

    for part in (0, 1):
        for way in (0, 1):
            go(kv_copies[way, 1, part])
    wz_down()
    go(q_copies[1])
    go(q_copies[7])

    acc[...] = jnp.zeros_like(acc)
    seg_copy.wait()
    row_iota = lax.broadcasted_iota(jnp.int32, (BLOCK, BLOCK), 0)
    col_iota = lax.broadcasted_iota(jnp.int32, (BLOCK, BLOCK), 1)
    for qi in range(RING):
        seg_rows = jnp.broadcast_to(seg[:, qi * BLOCK:(qi + 1) * BLOCK], (BLOCK, BLOCK)).T
        low_key = max(0, qi - 4)
        for kj in range(low_key, qi + 1):
            allowed = seg_rows == seg[:, kj * BLOCK:(kj + 1) * BLOCK]
            if kj == qi:
                allowed = allowed & (col_iota <= row_iota)
            bias[qi, :, (kj - low_key) * BLOCK:(kj - low_key + 1) * BLOCK] = jnp.where(allowed, 0.0, MASKED)

    kv_pass(1)
    go(q_copies[2])
    go(q_copies[6])
    wz_up(1)
    kv_pass(2)
    go(q_copies[3])
    go(q_copies[5])
    wz_wait(0)

    @pl.when(beside)
    def _():
        pl.semaphore_wait(x_ready, 1)

    @pl.when(core == 1)
    def _():
        pl.semaphore_wait(sib_ready, 1)

    wx_first(0)
    wz_up(2)
    kv_pass(3)
    go(q_copies[4])
    wz_wait(1)
    wx_first(1)
    wz_up(3)
    kv_pass(4)
    wx_pass(1, 0)
    wz_wait(2)
    wx_first(2)
    k_in.wait()
    v_in.wait()
    q_in.wait()
    for copy in q_copies.values():
        copy.wait_recv()

    def attend(qi):
        low_key = max(0, qi - 4)
        count = (qi + 1 - low_key) * BLOCK
        keys = kv[low_key:qi + 1, 0].reshape(count, HEAD_DIM)
        vals = kv[low_key:qi + 1, 1].reshape(count, HEAD_DIM)
        scores = lax.dot_general(qbuf[qi], keys, (((1,), (1,)), ((), ())), preferred_element_type=F32)
        scores = scores * (HEAD_DIM ** -0.5 * LOG2_E) + bias[qi, :, :count]
        top = jnp.max(scores, axis=1, keepdims=True)
        probs = jnp.exp2(scores - top)
        total = jnp.sum(probs, axis=1, keepdims=True)
        heads_out = jnp.dot(probs.astype(BF16), vals, preferred_element_type=F32) / total
        astage[qi // 2, (qi % 2) * BLOCK:(qi % 2 + 1) * BLOCK, :] = heads_out.astype(BF16)

    own_copy = pltpu.make_async_copy(astage.at[z], aall.at[y, z], local_sem.at[5])

    def az_copy(b):
        return remote(astage.at[b], aall.at[y, z], az_s.at[b], az_r.at[z], at_z(b))

    for b in range(GROUP):
        attend(2 * b)
        attend(2 * b + 1)

        @pl.when(z == b)
        def _():
            own_copy.start()

        @pl.when(z != b)
        def _():
            az_copy(b).start()

        if b == 1:
            wx_pass(1, 1)

    def ay_copy(way, hop, sub):
        block = ring(y - hop + 1) if way == 0 else ring(y + hop - 1)
        part = aall.at[block, sources[sub]]
        return remote(part, part, ay_s.at[way, hop - 1, sub], ay_r.at[way, hop - 1, sub], at_y(1 if way == 0 else -1))

    ay_copies = {
        (way, hop, sub): ay_copy(way, hop, sub)
        for way in (0, 1) for hop in (1, 2, 3, 4) for sub in range(4)
        if hop < 4 or sub // 2 == way
    }

    def ay_first(sub):
        if sub == 0:
            own_copy.wait()
        else:
            remote(astage.at[0], aall.at[y, sources[sub]], az_s.at[0], az_r.at[sources[sub]], sibling).wait_recv()
        go(ay_copies[0, 1, sub])
        go(ay_copies[1, 1, sub])

    def ay_pass(hop, sub):
        for way in (0, 1):
            ay_copies[way, hop, sub].wait_recv()
            if (way, hop + 1, sub) in ay_copies:
                go(ay_copies[way, hop + 1, sub])

    def apart(there, here):
        ahead = lax.rem(there - here + RING, RING)
        return jnp.minimum(ahead, RING - ahead)

    def project(reach, before):
        def one(block, carry):
            far = jnp.maximum(apart(block, y), apart(block, x))

            @pl.when((far <= reach) & (far > before))
            def _():
                left = jnp.concatenate([aall[block, g] for g in range(GROUP)], axis=1)
                for tile in range(4):
                    cols = slice(tile * 256, (tile + 1) * 256)
                    right = wall[block, :, :, cols].reshape(GROUP * BLOCK, 256)
                    acc[:, cols] += jnp.dot(left, right, preferred_element_type=F32)

            return carry

        lax.fori_loop(0, RING, one, 0)

    ay_first(0)
    wx_pass(1, 2)
    ay_first(1)
    ay_pass(1, 0)
    wx_pass(2, 0)
    ay_first(2)
    ay_pass(1, 1)
    wx_pass(2, 1)
    ay_pass(2, 0)
    ay_pass(1, 2)
    wx_pass(2, 2)
    ay_first(3)
    hid_start()
    ay_pass(2, 1)
    wx_pass(3, 0)
    ay_pass(2, 2)
    ay_pass(3, 0)
    ay_pass(1, 3)
    wx_pass(3, 1)
    ay_pass(3, 1)
    ay_pass(2, 3)
    wx_pass(3, 2)
    ay_pass(3, 2)
    ay_pass(3, 3)
    w_in.wait()
    sib_wait((0, 1, 2, 3, 4))
    project(2, -1)
    wx_last()
    sib_wait((5, 6))
    project(3, 2)
    for sub in range(4):
        ay_copies[sub // 2, 4, sub].wait_recv()
    sib_wait((7,))
    project(4, 3)

    @pl.when(p == 0)
    def _():
        pltpu.make_async_copy(emb_ref, hbuf, local_sem.at[4]).wait()

    @pl.when(p > 0)
    def _():
        for copy in hid_copies:
            copy.wait_recv()

    out_ref[...] = (hbuf[...].astype(F32) + acc[...]).astype(BF16)

    for copy in sends:
        copy.wait_send()
    for b in range(GROUP):
        @pl.when(z != b)
        def _():
            az_copy(b).wait_send()
            wz_copy(b).wait_send()

    @pl.when(p < 31)
    def _():
        for copy in hid_copies:
            copy.wait_send()


def on_device(queries, keys, values, seg_ids, out_weight, embedded, hidden_prev):
    rows, width = embedded.shape
    dma = pltpu.SemaphoreType.DMA
    hbm = pl.BlockSpec(memory_space=pltpu.HBM)
    vmem = pl.BlockSpec(memory_space=pltpu.VMEM)
    operands = (
        queries[0], keys[0], values[0], seg_ids,
        out_weight.reshape(RING, BLOCK, out_weight.shape[1]), embedded, hidden_prev[0],
    )
    result = pl.pallas_call(
        kernel,
        out_shape=jax.ShapeDtypeStruct((rows, width), BF16),
        in_specs=[hbm] * 7,
        out_specs=vmem,
        scratch_shapes=[
            pltpu.VMEM((1, RING * BLOCK), jnp.int32),
            pltpu.VMEM((RING, BLOCK, HEAD_DIM), BF16),
            pltpu.VMEM((RING, 2, BLOCK, HEAD_DIM), BF16),
            pltpu.VMEM((RING, BLOCK, 5 * BLOCK), F32),
            pltpu.VMEM((GROUP, 2 * BLOCK, HEAD_DIM), BF16),
            pltpu.VMEM((RING, GROUP, 2 * BLOCK, HEAD_DIM), BF16),
            pltpu.VMEM((RING, GROUP, BLOCK, width), BF16),
            pltpu.VMEM((rows, width), BF16),
            pltpu.VMEM((rows, width), F32),
            pltpu.SemaphoreType.REGULAR((GROUP,)), pltpu.SemaphoreType.REGULAR,
            pltpu.SemaphoreType.REGULAR, pltpu.SemaphoreType.REGULAR,
            dma((7,)),
            dma((2, 4, 2)), dma((2, 4, 2)),
            dma((8,)), dma((8,)),
            dma((4,)), dma((4,)),
            dma((2, 4, 3)), dma((2, 4, 3)),
            dma((8, 3)), dma((8, 3)),
            dma((4,)), dma((4,)),
            dma((4,)), dma((4,)),
            dma((2, 4, 4)), dma((2, 4, 4)),
        ],
        compiler_params=pltpu.CompilerParams(
            collective_id=0, has_side_effects=True, vmem_limit_bytes=48 * 1024 * 1024
        ),
    )(*(pltpu.with_memory_space_constraint(operand, pltpu.HBM) for operand in operands))
    return result[None]


def solution(mesh):
    return jax.shard_map(
        on_device,
        mesh=mesh,
        in_specs=(
            P("phase", "ctx", "tp"),
            P("phase", "ctx", "tp"),
            P("phase", "ctx", "tp"),
            P("phase", None),
            P("tp", "ctx"),
            P("tp", "ctx"),
            P("phase", "tp", "ctx"),
        ),
        out_specs=P("phase", "tp", "ctx"),
        check_vma=False,
    )
```

```python
import jax
import jax.numpy as jnp
from jax import lax
from jax.experimental import pallas as pl
from jax.experimental.pallas import tpu as pltpu
from jax.sharding import PartitionSpec as P

HEAD_DIM = 128
BLOCK = 128
RING = 8
GROUP = 4
PIECE = 64
MASKED = -1e30
LOG2_E = 1.4426950408889634
F32 = jnp.float32
BF16 = jnp.bfloat16


def kernel(
    q_ref, k_ref, v_ref, seg_in, w_ref, emb_ref, hp_ref, out_ref,
    seg, qbuf, kv, bias, astage, aall, wall, hbuf, acc,
    ready, hid_ready, x_ready, sib_ready, local_sem, kv_s, kv_r, q_s, q_r, wz_s, wz_r, wx_s, wx_r, sib_s, sib_r, hid_s, hid_r, az_s, az_r, ay_s, ay_r,
):
    p = lax.axis_index("phase")
    y = lax.axis_index("ctx")
    z = lax.axis_index("tp")
    x = lax.div(p, 4)
    zh = lax.rem(lax.div(p, 2), 2)
    core = lax.rem(p, 2)

    def ring(value):
        return lax.rem(value + 2 * RING, RING)

    def at_y(step):
        return {"phase": p, "ctx": ring(y + step), "tp": z}

    def at_x(step):
        return {"phase": lax.rem(p + 4 * step + 32, 32), "ctx": y, "tp": z}

    def at_z(place):
        return {"phase": p, "ctx": y, "tp": place}

    def at_phase(step):
        return {"phase": lax.rem(p + step + 32, 32), "ctx": y, "tp": z}

    sibling = {"phase": p + 1 - 2 * core, "ctx": y, "tp": z}

    def remote(src, dst, send, recv, where):
        return pltpu.make_async_remote_copy(
            src_ref=src, dst_ref=dst, send_sem=send, recv_sem=recv,
            device_id=where, device_id_type=pl.DeviceIdType.MESH,
        )

    def signal(sem, where):
        pl.semaphore_signal(sem, inc=1, device_id=where, device_id_type=pl.DeviceIdType.MESH)

    barrier = pltpu.get_barrier_semaphore()
    lane = y + z + zh + core
    tail = (lane == 0) & (x == 0)
    beside = (lane == 0) & ((x == 1) | (x == RING - 1))
    for peer in (at_y(1), at_y(-1)):
        signal(barrier, peer)

    @pl.when(jnp.logical_not(tail))
    def _():
        for peer in (at_x(1), at_x(-1)):
            signal(barrier, peer)

    @pl.when(core == 1)
    def _():
        signal(barrier, sibling)

    for d in range(1, GROUP):
        @pl.when(z + d < GROUP)
        def _():
            signal(barrier, at_z(z + d))

    @pl.when(zh == 0)
    def _():
        signal(barrier, at_phase(2 * core - 1))

    k_in = pltpu.make_async_copy(k_ref, kv.at[y, 0], local_sem.at[0])
    v_in = pltpu.make_async_copy(v_ref, kv.at[y, 1], local_sem.at[1])
    q_in = pltpu.make_async_copy(
        q_ref.at[:, pl.ds(pl.multiple_of(y * HEAD_DIM, HEAD_DIM), HEAD_DIM)], qbuf.at[y], local_sem.at[2]
    )
    w_in = pltpu.make_async_copy(w_ref, wall.at[:, z], local_sem.at[3])
    k_in.start()
    v_in.start()
    q_in.start()
    seg_copy = pltpu.make_async_copy(seg_in, seg, local_sem.at[6])
    seg_copy.start()
    w_in.start()

    @pl.when(p == 0)
    def _():
        pltpu.make_async_copy(emb_ref, hbuf, local_sem.at[4]).start()

    awaited = 5 - core + z + zh - jnp.where(beside, 1, 0)
    pl.semaphore_wait(barrier, awaited)

    @pl.when(tail)
    def _():
        for peer in (at_x(1), at_x(-1)):
            signal(x_ready, peer)

    @pl.when(core == 0)
    def _():
        signal(sib_ready, sibling)

    for d in range(1, GROUP):
        @pl.when(z - d >= 0)
        def _():
            signal(ready.at[z], at_z(z - d))

    @pl.when((zh == 1) & (core == 0))
    def _():
        signal(hid_ready, at_phase(-1))

    sends = []

    def go(copy):
        copy.start()
        sends.append(copy)

    def kv_copy(way, hop, part):
        block = ring(y - hop + 1) if way == 0 else ring(y + hop - 1)
        held = kv.at[block, part]
        return remote(
            held if hop > 1 else (k_ref, v_ref)[part], held, kv_s.at[way, hop - 1, part], kv_r.at[way, hop - 1, part], at_y(1 if way == 0 else -1)
        )

    kv_copies = {
        (way, hop, part): kv_copy(way, hop, part)
        for way in (0, 1) for hop in (1, 2, 3, 4) for part in (0, 1)
        if hop < 4 or part == way
    }

    def kv_pass(hop):
        for part in (0, 1):
            for way in (0, 1):
                if (way, hop, part) in kv_copies:
                    kv_copies[way, hop, part].wait_recv()
                if (way, hop + 1, part) in kv_copies:
                    go(kv_copies[way, hop + 1, part])

    piece = pl.ds(pl.multiple_of(core * PIECE, PIECE), PIECE)
    half = PIECE // 2
    low = pl.ds(pl.multiple_of(core * PIECE, half), half)
    high = pl.ds(pl.multiple_of(core * PIECE + half, half), half)
    first = jnp.abs(z - 1)
    last = 3 - 3 * lax.div(z, 3)
    others = [first, 6 - z - first - last, last]
    sources = [z] + others

    def wz_copy(there):
        return remote(w_ref.at[x, piece], wall.at[x, z, piece], wz_s.at[there], wz_r.at[z], at_z(there))

    def wz_down():
        for d in range(1, GROUP):
            @pl.when(z - d >= 0)
            def _():
                wz_copy(z - d).start()

    def wz_up(d):
        @pl.when(z + d < GROUP)
        def _():
            pl.semaphore_wait(ready.at[z + d], 1)
            wz_copy(z + d).start()

    def wz_wait(sub):
        held = wall.at[x, others[sub], piece]
        remote(held, held, wz_s.at[others[sub]], wz_r.at[others[sub]], sibling).wait_recv()

    def wx_copy(way, hop, sub):
        block = ring(x - hop + 1) if way == 0 else ring(x + hop - 1)
        rows = piece
        if hop == 4 and sub == 2:
            rows = low if way == 0 else high
        part = wall.at[block, others[sub], rows]
        return remote(part, part, wx_s.at[way, hop - 1, sub], wx_r.at[way, hop - 1, sub], at_x(1 if way == 0 else -1))

    wx_copies = {
        (way, hop, sub): wx_copy(way, hop, sub)
        for way in (0, 1) for hop in (1, 2, 3, 4) for sub in (0, 1, 2)
        if hop < 4 or sub == 2 or sub == way
    }

    def sib_copy(slot, sub):
        hop = (slot + 1) // 2
        block = ring(x - hop) if slot % 2 else ring(x + hop)
        part = wall.at[block, others[sub], piece]
        return remote(part, part, sib_s.at[slot, sub], sib_r.at[slot, sub], sibling)

    sib_copies = {(slot, sub): sib_copy(slot, sub) for slot in range(8) for sub in range(3)}

    def wx_first(sub):
        go(wx_copies[0, 1, sub])
        go(wx_copies[1, 1, sub])
        go(sib_copies[0, sub])

    def wx_pass(hop, sub):
        for way in (0, 1):
            wx_copies[way, hop, sub].wait_recv()
            if (way, hop + 1, sub) in wx_copies:
                go(wx_copies[way, hop + 1, sub])
            go(sib_copies[2 * hop - 1 + way, sub])

    def wx_last():
        for sub in (0, 1, 2):
            for way in (0, 1):
                if (way, 4, sub) in wx_copies:
                    wx_copies[way, 4, sub].wait_recv()
            go(sib_copies[7, sub])

    def sib_wait(slots):
        for slot in slots:
            for sub in range(3):
                sib_copies[slot, sub].wait_recv()

    def hid_copy(part):
        rows = pl.ds(part * PIECE, PIECE)
        return remote(hp_ref.at[rows], hbuf.at[rows], hid_s.at[part], hid_r.at[part], at_phase(1))

    hid_copies = [hid_copy(part) for part in range(4)]

    def hid_start(half):
        if half == 0:
            @pl.when((zh == 0) & (core == 1))
            def _():
                pl.semaphore_wait(hid_ready, 1)

        @pl.when((zh == half) & (p < 31))
        def _():
            for copy in hid_copies:
                copy.start()

    def q_copy(step):
        there = ring(y + step)
        return remote(
            q_ref.at[:, pl.ds(pl.multiple_of(there * HEAD_DIM, HEAD_DIM), HEAD_DIM)],
            qbuf.at[y], q_s.at[step], q_r.at[step], at_y(step),
        )

    q_copies = {step: q_copy(step) for step in range(1, RING)}

    for part in (0, 1):
        for way in (0, 1):
            go(kv_copies[way, 1, part])
    wz_down()
    go(q_copies[1])
    go(q_copies[7])

    acc[...] = jnp.zeros_like(acc)
    seg_copy.wait()
    row_iota = lax.broadcasted_iota(jnp.int32, (BLOCK, BLOCK), 0)
    col_iota = lax.broadcasted_iota(jnp.int32, (BLOCK, BLOCK), 1)
    for qi in range(RING):
        seg_rows = jnp.broadcast_to(seg[:, qi * BLOCK:(qi + 1) * BLOCK], (BLOCK, BLOCK)).T
        low_key = max(0, qi - 4)
        for kj in range(low_key, qi + 1):
            allowed = seg_rows == seg[:, kj * BLOCK:(kj + 1) * BLOCK]
            if kj == qi:
                allowed = allowed & (col_iota <= row_iota)
            bias[qi, :, (kj - low_key) * BLOCK:(kj - low_key + 1) * BLOCK] = jnp.where(allowed, 0.0, MASKED)

    kv_pass(1)
    go(q_copies[2])
    go(q_copies[6])
    wz_up(1)
    kv_pass(2)
    go(q_copies[3])
    go(q_copies[5])
    wz_wait(0)

    @pl.when(beside)
    def _():
        pl.semaphore_wait(x_ready, 1)

    @pl.when(core == 1)
    def _():
        pl.semaphore_wait(sib_ready, 1)

    wx_first(0)
    wz_up(2)
    kv_pass(3)
    go(q_copies[4])
    wz_wait(1)
    wx_first(1)
    wz_up(3)
    kv_pass(4)
    wx_pass(1, 0)
    wz_wait(2)
    wx_first(2)
    k_in.wait()
    v_in.wait()
    q_in.wait()
    for copy in q_copies.values():
        copy.wait_recv()

    def attend(qi):
        low_key = max(0, qi - 4)
        count = (qi + 1 - low_key) * BLOCK
        keys = kv[low_key:qi + 1, 0].reshape(count, HEAD_DIM)
        vals = kv[low_key:qi + 1, 1].reshape(count, HEAD_DIM)
        scores = lax.dot_general(qbuf[qi], keys, (((1,), (1,)), ((), ())), preferred_element_type=F32)
        scores = scores * (HEAD_DIM ** -0.5 * LOG2_E) + bias[qi, :, :count]
        top = jnp.max(scores, axis=1, keepdims=True)
        probs = jnp.exp2(scores - top)
        total = jnp.sum(probs, axis=1, keepdims=True)
        heads_out = jnp.dot(probs.astype(BF16), vals, preferred_element_type=F32) / total
        astage[qi // 2, (qi % 2) * BLOCK:(qi % 2 + 1) * BLOCK, :] = heads_out.astype(BF16)

    own_copy = pltpu.make_async_copy(astage.at[z], aall.at[y, z], local_sem.at[5])

    def az_copy(b):
        return remote(astage.at[b], aall.at[y, z], az_s.at[b], az_r.at[z], at_z(b))

    for b in range(GROUP):
        attend(2 * b)
        attend(2 * b + 1)

        @pl.when(z == b)
        def _():
            own_copy.start()

        @pl.when(z != b)
        def _():
            az_copy(b).start()


    def ay_copy(way, hop, sub):
        block = ring(y - hop + 1) if way == 0 else ring(y + hop - 1)
        part = aall.at[block, sources[sub]]
        return remote(part, part, ay_s.at[way, hop - 1, sub], ay_r.at[way, hop - 1, sub], at_y(1 if way == 0 else -1))

    ay_copies = {
        (way, hop, sub): ay_copy(way, hop, sub)
        for way in (0, 1) for hop in (1, 2, 3, 4) for sub in range(4)
        if hop < 4 or sub // 2 == way
    }

    def ay_first(sub):
        if sub == 0:
            own_copy.wait()
        else:
            remote(astage.at[0], aall.at[y, sources[sub]], az_s.at[0], az_r.at[sources[sub]], sibling).wait_recv()
        go(ay_copies[0, 1, sub])
        go(ay_copies[1, 1, sub])

    def ay_pass(hop, sub):
        for way in (0, 1):
            ay_copies[way, hop, sub].wait_recv()
            if (way, hop + 1, sub) in ay_copies:
                go(ay_copies[way, hop + 1, sub])

    def apart(there, here):
        ahead = lax.rem(there - here + RING, RING)
        return jnp.minimum(ahead, RING - ahead)

    def project(reach, before):
        def one(block, carry):
            far = jnp.maximum(apart(block, y), apart(block, x))

            @pl.when((far <= reach) & (far > before))
            def _():
                left = jnp.concatenate([aall[block, g] for g in range(GROUP)], axis=1)
                for tile in range(4):
                    cols = slice(tile * 256, (tile + 1) * 256)
                    right = wall[block, :, :, cols].reshape(GROUP * BLOCK, 256)
                    acc[:, cols] += jnp.dot(left, right, preferred_element_type=F32)

            return carry

        lax.fori_loop(0, RING, one, 0)

    ay_first(0)
    wx_pass(1, 1)
    ay_first(1)
    wx_pass(1, 2)
    ay_pass(1, 0)
    ay_first(2)
    wx_pass(2, 0)
    ay_pass(1, 1)
    wx_pass(2, 1)
    ay_pass(2, 0)
    ay_pass(1, 2)
    wx_pass(2, 2)
    ay_first(3)
    hid_start(1)
    ay_pass(2, 1)
    wx_pass(3, 0)
    ay_pass(2, 2)
    ay_pass(3, 0)
    ay_pass(1, 3)
    hid_start(0)
    wx_pass(3, 1)
    ay_pass(3, 1)
    ay_pass(2, 3)
    wx_pass(3, 2)
    ay_pass(3, 2)
    ay_pass(3, 3)
    w_in.wait()
    sib_wait((0, 1, 2, 3, 4))
    project(2, -1)
    wx_last()
    sib_wait((5, 6))
    project(3, 2)
    for sub in range(4):
        ay_copies[sub // 2, 4, sub].wait_recv()
    sib_wait((7,))
    project(4, 3)

    @pl.when(p == 0)
    def _():
        pltpu.make_async_copy(emb_ref, hbuf, local_sem.at[4]).wait()

    @pl.when(p > 0)
    def _():
        for copy in hid_copies:
            copy.wait_recv()

    out_ref[...] = (hbuf[...].astype(F32) + acc[...]).astype(BF16)

    for copy in sends:
        copy.wait_send()
    for b in range(GROUP):
        @pl.when(z != b)
        def _():
            az_copy(b).wait_send()
            wz_copy(b).wait_send()

    @pl.when(p < 31)
    def _():
        for copy in hid_copies:
            copy.wait_send()


def on_device(queries, keys, values, seg_ids, out_weight, embedded, hidden_prev):
    rows, width = embedded.shape
    dma = pltpu.SemaphoreType.DMA
    hbm = pl.BlockSpec(memory_space=pltpu.HBM)
    vmem = pl.BlockSpec(memory_space=pltpu.VMEM)
    operands = (
        queries[0], keys[0], values[0], seg_ids,
        out_weight.reshape(RING, BLOCK, out_weight.shape[1]), embedded, hidden_prev[0],
    )
    result = pl.pallas_call(
        kernel,
        out_shape=jax.ShapeDtypeStruct((rows, width), BF16),
        in_specs=[hbm] * 7,
        out_specs=vmem,
        scratch_shapes=[
            pltpu.VMEM((1, RING * BLOCK), jnp.int32),
            pltpu.VMEM((RING, BLOCK, HEAD_DIM), BF16),
            pltpu.VMEM((RING, 2, BLOCK, HEAD_DIM), BF16),
            pltpu.VMEM((RING, BLOCK, 5 * BLOCK), F32),
            pltpu.VMEM((GROUP, 2 * BLOCK, HEAD_DIM), BF16),
            pltpu.VMEM((RING, GROUP, 2 * BLOCK, HEAD_DIM), BF16),
            pltpu.VMEM((RING, GROUP, BLOCK, width), BF16),
            pltpu.VMEM((rows, width), BF16),
            pltpu.VMEM((rows, width), F32),
            pltpu.SemaphoreType.REGULAR((GROUP,)), pltpu.SemaphoreType.REGULAR,
            pltpu.SemaphoreType.REGULAR, pltpu.SemaphoreType.REGULAR,
            dma((7,)),
            dma((2, 4, 2)), dma((2, 4, 2)),
            dma((8,)), dma((8,)),
            dma((4,)), dma((4,)),
            dma((2, 4, 3)), dma((2, 4, 3)),
            dma((8, 3)), dma((8, 3)),
            dma((4,)), dma((4,)),
            dma((4,)), dma((4,)),
            dma((2, 4, 4)), dma((2, 4, 4)),
        ],
        compiler_params=pltpu.CompilerParams(
            collective_id=0, has_side_effects=True, vmem_limit_bytes=48 * 1024 * 1024
        ),
    )(*(pltpu.with_memory_space_constraint(operand, pltpu.HBM) for operand in operands))
    return result[None]


def solution(mesh):
    return jax.shard_map(
        on_device,
        mesh=mesh,
        in_specs=(
            P("phase", "ctx", "tp"),
            P("phase", "ctx", "tp"),
            P("phase", "ctx", "tp"),
            P("phase", None),
            P("tp", "ctx"),
            P("tp", "ctx"),
            P("phase", "tp", "ctx"),
        ),
        out_specs=P("phase", "tp", "ctx"),
        check_vma=False,
    )
```
